32 devices in a mesh: inner: 8 (over z, y), cols: 4 (over x, core).
Axes of the slice: x: 2, y: 2, z: 4, core: 2. Of those that a mesh axis runs over, the one named last changes fastest.
Arguments:
- left_u: bfloat16 [64, 512, 128], P(('inner', 'cols')), may hold values from -6 to 6
- left_v: bfloat16 [64, 512, 128], P(('inner', 'cols')), may hold values from -0.0234375 to 0.0234375
- right_u: bfloat16 [16, 64, 512, 128], P('cols', 'inner'), may hold values from -6 to 6
- right_v: bfloat16 [16, 64, 512, 128], P('cols', 'inner'), may hold values from -0.1875 to 0.1875
- sketch: bfloat16 [16, 512, 128], P('cols'), may hold values from -0.25 to 0.25
- tile_index: int32 [16, 64], P('cols', 'inner'), may hold values from 0 to 63, as said below
- slot_mask: int32 [16, 64], P('cols', 'inner'), may hold values from 0 to 1, as said below
Outputs:
- basis: float32 [16, 512, 128], P('cols', 'inner')
- coeff: float32 [16, 512, 128], P('cols', 'inner')
The draws below stay inside these ranges and needn't reach their ends.
Inputs may be any that keep to these rules, and one draw needn't show every extreme that they name: `tile_index`: slot s of an output tile belongs to inner group g = s // 8 and names a left tile of that group, g * 8 to g * 8 + 7; the tiles named by one output tile's slots of one group are distinct. `slot_mask`: in each output tile and inner group the live slots come first and there is at least one; in every output tile some group has all 8 slots live, and the others at most 4.
All inputs are finite; a program needn't handle non-finite values.
Results may differ from the reference program's by a relative error of at most 0.0045.
Values may be sent and summed in bfloat16 or wider, within the bound.
A program may use at most 64 MiB of HBM per device.

```python
import math
import jax
import jax.numpy as jnp
from jax import lax

NB = 512
R = 128
SLOTS = 8
OUT = 16
LISTS = 64
TILES = 64


def draw_tile_index(key, part):
    groups = LISTS // SLOTS
    keys = jax.random.split(jax.random.fold_in(key, 11), OUT * groups)
    orders = jax.vmap(lambda sub_key: jax.random.permutation(sub_key, SLOTS))(keys)
    orders = orders.reshape(OUT, groups, SLOTS).astype(jnp.int32)
    offsets = (jnp.arange(groups, dtype=jnp.int32) * SLOTS)[None, :, None]
    return (orders + offsets).reshape(OUT, LISTS).astype(jnp.int32)


def draw_slot_mask(key, part):
    groups = LISTS // SLOTS
    first_key, second_key = jax.random.split(jax.random.fold_in(key, 23))
    counts = jax.random.randint(first_key, (OUT, groups), 1, SLOTS // 2 + 1)
    busiest = jax.random.randint(second_key, (OUT,), 0, groups)
    counts = jnp.where(jnp.arange(groups)[None, :] == busiest[:, None], SLOTS, counts)
    filled = jnp.arange(SLOTS)[None, None, :] < counts[:, :, None]
    return filled.astype(jnp.int32).reshape(OUT, LISTS)


def level_of(stream_key, extent, shards, smallest, high):
    gain, own = 1.0, jax.random.fold_in(stream_key, 6)
    for position, blocks in shards:
        heights = jnp.exp(jax.random.uniform(jax.random.fold_in(own, position), (blocks,), jnp.float32, smallest / len(shards), high / len(shards)))
        gain = gain * jnp.repeat(heights, extent[position] // blocks).reshape([-1 if axis == position else 1 for axis in range(len(extent))])
    return gain


def gaussian(stream_key, extent, width, reach, cuts=(), kind=jnp.bfloat16):
    array = jax.random.normal(stream_key, extent, jnp.float32) * width
    if len(cuts) > 0:
        array = level_of(stream_key, extent, cuts, -0.22, 0.18) * array
    return jnp.clip(array, min=-reach, max=reach).astype(kind)


def setup_inputs(seed: int = 0) -> dict:
    key_list = jax.random.split(jax.random.key(seed), 8)
    return {
        "left_u": gaussian(key_list[0], (TILES, NB, R), 1.0, 6.0, ((0, 32),)),
        "left_v": gaussian(key_list[1], (TILES, NB, R), (R * NB) ** -0.5, 0.0234375, ((0, 32),)),
        "right_u": gaussian(key_list[2], (OUT, LISTS, NB, R), 1.0, 6.0, ((0, 4), (1, 8))),
        "right_v": gaussian(key_list[3], (OUT, LISTS, NB, R), (R * LISTS // SLOTS) ** -0.5, 0.1875, ((0, 4), (1, 8))),
        "sketch": gaussian(key_list[4], (OUT, NB, R), NB ** -0.5, 0.25, ((0, 4),)),
        "tile_index": draw_tile_index(jax.random.fold_in(key_list[7], 71), 0),
        "slot_mask": draw_slot_mask(jax.random.fold_in(key_list[7], 71), 0),
    }


HIGH = lax.Precision.HIGHEST

def one_tile(left_u, left_v, right_ub, right_vb, sketch_j, index_j, mask_j):
    live_mask = mask_j.astype(jnp.float32)
    tile_u = jnp.take(left_u, index_j, axis=0).astype(jnp.float32)
    tile_v = jnp.take(left_v, index_j, axis=0).astype(jnp.float32)
    right_uf = right_ub.astype(jnp.float32)
    right_vf = right_vb.astype(jnp.float32)
    pairing = jnp.einsum('sna,snb->sab', tile_v, right_uf, precision=HIGH)
    probe = jnp.einsum('snb,nt->sbt', right_vf, sketch_j.astype(jnp.float32), precision=HIGH)
    mixing = (live_mask[:, None, None] * jnp.einsum('sab,sbt->sat', pairing, probe, precision=HIGH)).astype(jnp.bfloat16)
    sketched = jnp.einsum('sna,sat->nt', tile_u, mixing.astype(jnp.float32), precision=HIGH)
    gram_mat = jnp.dot(sketched.T, sketched, precision=HIGH)
    factor = jnp.linalg.cholesky(gram_mat)
    ortho = jax.scipy.linalg.solve_triangular(factor, sketched.T, lower=True).T
    basis = ortho * math.sqrt(NB)
    ortho_b = ortho.astype(jnp.bfloat16)
    projected = jnp.einsum('sna,nt->sat', tile_u, ortho_b.astype(jnp.float32), precision=HIGH)
    backward = (live_mask[:, None, None] * jnp.einsum('sab,sat->sbt', pairing, projected, precision=HIGH)).astype(jnp.bfloat16)
    coeff = jnp.einsum('snb,sbt->nt', right_vf, backward.astype(jnp.float32), precision=HIGH)
    return (basis, coeff)

def reference(left_u, left_v, right_u, right_v, sketch, tile_index, slot_mask):

    def per_tile(items):
        return one_tile(left_u, left_v, items[0], items[1], items[2], items[3], items[4])
    basis, coeff = lax.map(per_tile, (right_u, right_v, sketch, tile_index, slot_mask))
    return (basis, coeff)
```

```python
import functools
import math

import jax
import jax.numpy as jnp
from jax import lax
from jax.experimental import pallas as pl
from jax.experimental.pallas import tpu as pltpu
from jax.sharding import PartitionSpec as P

MESH = pl.DeviceIdType.MESH
F32 = jnp.float32
BF16 = jnp.bfloat16
NN = (((1,), (0,)), ((), ()))
NT = (((1,), (1,)), ((), ()))
TN = (((0,), (0,)), ((), ()))


def mm(a, b, dims):
    return lax.dot_general(a, b, dims, preferred_element_type=F32)


def split(a):
    hi = a.astype(BF16)
    return hi, (a - hi.astype(F32)).astype(BF16)


def mm_f32(a, b, dims):
    return lax.dot_general(a, b, dims, precision=lax.Precision.HIGHEST, preferred_element_type=F32)


def kernel(
    n_in, n_co, left_u, left_v, right_u, right_v, sketch, index, mask, basis, coeff,
    ug, vg, vt, ru, rv, sk, phi, plo, mix, ybuf, sbuf, r1, s2f, s2b, r2, yrow, yb,
    cbuf, csbuf, cr1, cs2f, cs2b, cr2, crow, xm, scale,
    load_sem, gs_sem, gr_sem, rs_send, rs_recv, ag_send, ag_recv,
):
    nx = n_co // 2
    ny = nx
    nz = n_in // ny
    tpd = left_u.shape[0]
    tiles = tpd * n_co
    n_out, slots, nb, rk = right_u.shape
    rows = nb // n_in
    me_in = lax.axis_index("inner")
    me_co = lax.axis_index("cols")
    x, core = lax.div(me_co, 2), lax.rem(me_co, 2)
    z, y = lax.div(me_in, ny), lax.rem(me_in, ny)

    def co_at(dx):
        return lax.rem(x + dx, nx) * 2 + core

    partner = x * 2 + (1 - core)

    def z_at(dz):
        return lax.rem(z + dz, nz) * ny + y

    def y_at(dy):
        return z * ny + lax.rem(y + dy, ny)

    sends = []

    def remote(src, dst, s_sem, r_sem, **dev):
        return pltpu.make_async_remote_copy(
            src_ref=src, dst_ref=dst, send_sem=s_sem, recv_sem=r_sem,
            device_id=dev, device_id_type=MESH,
        )

    def go(copy):
        copy.start()
        sends.append(copy)

    loads = []
    for j in range(n_out):
        for num, (src, dst) in enumerate(((sketch, sk), (right_v, rv), (right_u, ru))):
            loads.append(pltpu.make_async_copy(src.at[j], dst.at[j], load_sem.at[j, num]))
    own = pl.ds(me_co * tpd, tpd)
    own_v = pltpu.make_async_copy(left_v, vg.at[own], load_sem.at[n_out, 0])
    own_u = pltpu.make_async_copy(left_u, ug.at[own], load_sem.at[n_out, 1])
    for c in [own_v, own_u] + loads:
        c.start()

    barrier = pltpu.get_barrier_semaphore()
    for dx in range(1, nx):
        pl.semaphore_signal(barrier, inc=1, device_id={"cols": co_at(dx)}, device_id_type=MESH)
    pl.semaphore_signal(barrier, inc=1, device_id={"cols": partner}, device_id_type=MESH)
    for dy in range(1, ny):
        pl.semaphore_signal(barrier, inc=1, device_id={"inner": y_at(dy)}, device_id_type=MESH)
    for dz in range(1, nz):
        pl.semaphore_signal(barrier, inc=1, device_id={"inner": z_at(dz)}, device_id_type=MESH)
    pl.semaphore_wait(barrier, nx - 1 + 1 + ny - 1 + nz - 1)

    for num, (src, dst) in enumerate(((left_v, vg), (left_u, ug))):
        for dx in range(1, nx):
            go(remote(src, dst.at[own], gs_sem.at[num, dx], gr_sem.at[num, dx], cols=co_at(dx)))
        go(remote(src, dst.at[own], gs_sem.at[num, 0], gr_sem.at[num, 0], cols=partner))

    def block(dst, position):
        return dst.at[pl.ds(position * tpd, tpd)]

    def forward(num, dst):
        for dx in range(1, nx):
            part = block(dst, co_at(nx - dx))
            remote(part, part, gs_sem.at[num, dx], gr_sem.at[num, dx], cols=partner).wait_recv()
            go(remote(part, part, gs_sem.at[num, nx + dx], gr_sem.at[num, nx + dx], cols=partner))

    def gathered(num, dst):
        part = block(dst, partner)
        remote(part, part, gs_sem.at[num, 0], gr_sem.at[num, 0], cols=partner).wait_recv()
        for dx in range(1, nx):
            part = block(dst, lax.rem(x + nx - dx, nx) * 2 + (1 - core))
            remote(part, part, gs_sem.at[num, nx + dx], gr_sem.at[num, nx + dx], cols=partner).wait_recv()

    for c in loads:
        c.wait()
    forward(0, vg)
    gathered(0, vg)
    own_v.wait()
    own_u.wait()

    @pl.loop(0, tiles)
    def _(t):
        vt[t] = jnp.transpose(vg[t])

    for j in range(n_out):
        om = jnp.transpose(sk[j])

        @pl.loop(0, slots)
        def _(s, j=j, om=om):
            k = lax.rem(index[j, s], tiles)
            live = mask[j, s].astype(F32)
            probe_hi, probe_lo = split(mm(om, rv[j, s], NN))
            pair_hi, pair_lo = split(mm(vt[k], ru[j, s], NN))
            phi[j, s] = pair_hi
            plo[j, s] = pair_lo
            mixed = mm(pair_hi, probe_hi, NT) + mm(pair_hi, probe_lo, NT) + mm(pair_lo, probe_hi, NT)
            mix[j, s] = (mixed * live).astype(BF16)

        if j == 0:
            forward(1, ug)

    gathered(1, ug)

    def scatter_first(phase, j, total, buf, sb, first):
        buf[j] = total.reshape(nz, ny, rows, rk)
        low = total.astype(BF16).reshape(nz, ny, rows, rk)
        for yy in range(ny):
            sb[j, yy] = low[:, yy]
        for dy in range(1, ny):
            go(remote(
                sb.at[j, lax.rem(y + dy, ny)], first.at[j, dy],
                rs_send.at[phase, j, dy], rs_recv.at[phase, j, dy], inner=y_at(dy),
            ))

    def scatter_second(phase, j, buf, sb, first, sumf, sumb, second):
        total = buf[j, :, y]
        for dy in range(1, ny):
            part = first.at[j, dy]
            remote(part, part, rs_send.at[phase, j, dy], rs_recv.at[phase, j, dy], inner=y_at(dy)).wait_recv()
            total = total + first[j, dy].astype(F32)
        sumf[j] = total
        sumb[j] = total.astype(BF16)
        for dz in range(1, nz):
            go(remote(
                sumb.at[j, lax.rem(z + dz, nz)], second.at[j, dz],
                rs_send.at[phase, j, ny + dz], rs_recv.at[phase, j, ny + dz], inner=z_at(dz),
            ))

    def scatter_last(phase, j, sumf, second):
        total = sumf[j, z]
        for dz in range(1, nz):
            part = second.at[j, dz]
            remote(part, part, rs_send.at[phase, j, ny + dz], rs_recv.at[phase, j, ny + dz], inner=z_at(dz)).wait_recv()
            total = total + second[j, dz].astype(F32)
        return total

    for j in range(n_out):
        total = mm(ug[lax.rem(index[j, 0], tiles)], mix[j, 0], NN)
        for s in range(1, slots):
            total = total + mm(ug[lax.rem(index[j, s], tiles)], mix[j, s], NN)
        scatter_first(0, j, total, ybuf, sbuf, r1)
    for j in range(n_out):
        scatter_second(0, j, ybuf, sbuf, r1, s2f, s2b, r2)

    for j in range(n_out):
        total = scatter_last(0, j, s2f, r2)
        yrow[j] = total
        yb[j, me_in] = total.astype(BF16)
        part = yb.at[j, me_in]
        for dz in range(1, nz):
            go(remote(part, part, ag_send.at[j, 0, dz], ag_recv.at[j, 0, dz], inner=z_at(dz)))
        for dy in range(1, ny):
            go(remote(part, part, ag_send.at[j, dy, 0], ag_recv.at[j, dy, 0], inner=y_at(dy)))
    for j in range(n_out):
        for dz in range(1, nz):
            part = yb.at[j, z_at(nz - dz)]
            remote(part, part, ag_send.at[j, 0, dz], ag_recv.at[j, 0, dz], inner=z_at(dz)).wait_recv()
            for dy in range(1, ny):
                go(remote(part, part, ag_send.at[j, dy, dz], ag_recv.at[j, dy, dz], inner=y_at(dy)))

    for j in range(n_out):
        for dy in range(1, ny):
            for dz in range(nz):
                pos = lax.rem(z + nz - dz, nz) * ny + lax.rem(y + ny - dy, ny)
                part = yb.at[j, pos]
                remote(part, part, ag_send.at[j, dy, dz], ag_recv.at[j, dy, dz], inner=y_at(dy)).wait_recv()
        summed_t = jnp.transpose(yb[j].reshape(nb, rk))

        def step(s, total, j=j, summed_t=summed_t):
            live = mask[j, s].astype(F32)
            z_hi, z_lo = split(mm(summed_t, ug[lax.rem(index[j, s], tiles)], NN))
            back = mm(z_hi, phi[j, s], NN) + mm(z_hi, plo[j, s], NN) + mm(z_lo, phi[j, s], NN)
            b_hi, b_lo = split(back * live)
            return total + (mm(rv[j, s], b_hi, NT) + mm(rv[j, s], b_lo, NT))

        total = lax.fori_loop(0, slots, step, jnp.zeros((nb, rk), F32))
        scatter_first(1, j, total, cbuf, csbuf, cr1)

    row_id = lax.broadcasted_iota(jnp.int32, (rk, rk), 0)
    col_id = lax.broadcasted_iota(jnp.int32, (rk, rk), 1)
    lane = lax.broadcasted_iota(jnp.int32, (1, rk), 1)
    for j in range(n_out):
        summed = yb[j].reshape(nb, rk)
        gram = mm(summed, summed, TN)
        diag = jnp.where(row_id == col_id, gram, 0.0)
        s_row = lax.rsqrt(jnp.sum(diag, axis=0, keepdims=True))
        s_col = lax.rsqrt(jnp.sum(diag, axis=1, keepdims=True))
        scale[j] = s_row
        xm[j] = gram * s_col * s_row

    def eliminate(start, stop):
        ids = lax.broadcasted_iota(jnp.int32, (rk - start, 1), 0) + start
        at = pl.ds(start, rk - start)

        @pl.loop(start, stop)
        def _(k):
            hot = lane == k
            for j in range(n_out):
                block_x = xm[j, at]
                row = xm[j, pl.ds(k, 1)]
                pivot = jnp.sum(jnp.where(hot, row, 0.0), axis=1, keepdims=True)
                col = jnp.sum(jnp.where(hot, block_x, 0.0), axis=1, keepdims=True)
                weight = jnp.where(ids > k, col * (1.0 / pivot), 0.0)
                xm[j, at] = block_x - weight * (row + jnp.where(hot, 1.0, 0.0))

    piece = rk // 8
    for b in range(3):
        eliminate(b * piece, (b + 1) * piece)
    for j in range(n_out):
        scatter_second(1, j, cbuf, csbuf, cr1, cs2f, cs2b, cr2)
    for b in range(3, 8):
        eliminate(b * piece, (b + 1) * piece)

    for j in range(n_out):
        work = xm[j]
        pivots = jnp.sum(jnp.where(row_id == col_id, work, 0.0), axis=1, keepdims=True)
        lower = jnp.where(col_id < row_id, work, jnp.where(row_id == col_id, 1.0, 0.0))
        inverse = lower * lax.rsqrt(pivots) * scale[j]
        basis[j] = mm_f32(yrow[j], inverse, NT) * math.sqrt(nb)
        coeff[j] = mm_f32(scatter_last(1, j, cs2f, cr2), inverse, NT)

    for copy in sends:
        copy.wait_send()


def body(n_in, n_co, left_u, left_v, right_u, right_v, sketch, tile_index, slot_mask):
    n_out, slots, nb, rk = right_u.shape
    tiles = left_u.shape[0] * n_co
    nx = n_co // 2
    ny = nx
    nz = n_in // ny
    rows = nb // n_in
    wire = [
        pltpu.VMEM((n_out, nz, ny, rows, rk), F32),
        pltpu.VMEM((n_out, ny, nz, rows, rk), BF16),
        pltpu.VMEM((n_out, ny, nz, rows, rk), BF16),
        pltpu.VMEM((n_out, nz, rows, rk), F32),
        pltpu.VMEM((n_out, nz, rows, rk), BF16),
        pltpu.VMEM((n_out, nz, rows, rk), BF16),
        pltpu.VMEM((n_out, rows, rk), F32),
    ]
    out = jax.ShapeDtypeStruct((n_out, rows, rk), F32)
    hbm = pl.BlockSpec(memory_space=pl.ANY)
    smem = pl.BlockSpec(memory_space=pltpu.SMEM)
    vmem = pl.BlockSpec(memory_space=pltpu.VMEM)
    return pl.pallas_call(
        functools.partial(kernel, n_in, n_co),
        out_shape=(out, out),
        in_specs=[hbm] * 5 + [smem] * 2,
        out_specs=(vmem, vmem),
        scratch_shapes=[
            pltpu.VMEM((tiles, nb, rk), BF16),
            pltpu.VMEM((tiles, nb, rk), BF16),
            pltpu.VMEM((tiles, rk, nb), BF16),
            pltpu.VMEM((n_out, slots, nb, rk), BF16),
            pltpu.VMEM((n_out, slots, nb, rk), BF16),
            pltpu.VMEM((n_out, nb, rk), BF16),
            pltpu.VMEM((n_out, slots, rk, rk), BF16),
            pltpu.VMEM((n_out, slots, rk, rk), BF16),
            pltpu.VMEM((n_out, slots, rk, rk), BF16),
        ]
        + wire
        + [pltpu.VMEM((n_out, n_in, rows, rk), BF16)]
        + wire
        + [
            pltpu.VMEM((n_out, rk, rk), F32),
            pltpu.VMEM((n_out, 1, rk), F32),
            pltpu.SemaphoreType.DMA((n_out + 1, 3)),
            pltpu.SemaphoreType.DMA((2, 2 * nx)),
            pltpu.SemaphoreType.DMA((2, 2 * nx)),
            pltpu.SemaphoreType.DMA((2, n_out, ny + nz)),
            pltpu.SemaphoreType.DMA((2, n_out, ny + nz)),
            pltpu.SemaphoreType.DMA((n_out, ny, nz)),
            pltpu.SemaphoreType.DMA((n_out, ny, nz)),
        ],
        compiler_params=pltpu.CompilerParams(
            collective_id=0, has_side_effects=True, vmem_limit_bytes=60 * 1024 * 1024
        ),
    )(left_u, left_v, right_u, right_v, sketch, tile_index, slot_mask)


def solution(mesh):
    return jax.shard_map(
        functools.partial(body, mesh.shape["inner"], mesh.shape["cols"]),
        mesh=mesh,
        in_specs=(
            P(("inner", "cols"), None, None),
            P(("inner", "cols"), None, None),
            P("cols", "inner", None, None),
            P("cols", "inner", None, None),
            P("cols", None, None),
            P("cols", "inner"),
            P("cols", "inner"),
        ),
        out_specs=(P("cols", "inner", None), P("cols", "inner", None)),
        check_vma=False,
    )
```

```python
import functools
import math

import jax
import jax.numpy as jnp
from jax import lax
from jax.experimental import pallas as pl
from jax.experimental.pallas import tpu as pltpu
from jax.sharding import PartitionSpec as P

MESH = pl.DeviceIdType.MESH
F32 = jnp.float32
BF16 = jnp.bfloat16
NN = (((1,), (0,)), ((), ()))
NT = (((1,), (1,)), ((), ()))
TN = (((0,), (0,)), ((), ()))


def mm(a, b, dims):
    return lax.dot_general(a, b, dims, preferred_element_type=F32)


def split(a):
    hi = a.astype(BF16)
    return hi, (a - hi.astype(F32)).astype(BF16)


def mm_f32(a, b, dims):
    return lax.dot_general(a, b, dims, precision=lax.Precision.HIGHEST, preferred_element_type=F32)


def kernel(
    n_in, n_co, left_u, left_v, right_u, right_v, sketch, index, mask, basis, coeff,
    ug, vg, vt, ru, rv, sk, phi, plo, mix, ybuf, sbuf, r1, s2f, s2b, r2, yrow, yb,
    cbuf, csbuf, cr1, cs2f, cs2b, cr2, crow, xm, scale, bt,
    load_sem, gs_sem, gr_sem, rs_send, rs_recv, ag_send, ag_recv,
):
    nx = n_co // 2
    ny = nx
    nz = n_in // ny
    tpd = left_u.shape[0]
    tiles = tpd * n_co
    n_out, slots, nb, rk = right_u.shape
    rows = nb // n_in
    me_in = lax.axis_index("inner")
    me_co = lax.axis_index("cols")
    x, core = lax.div(me_co, 2), lax.rem(me_co, 2)
    z, y = lax.div(me_in, ny), lax.rem(me_in, ny)

    def co_at(dx):
        return lax.rem(x + dx, nx) * 2 + core

    partner = x * 2 + (1 - core)

    def z_at(dz):
        return lax.rem(z + dz, nz) * ny + y

    def y_at(dy):
        return z * ny + lax.rem(y + dy, ny)

    sends = []

    def remote(src, dst, s_sem, r_sem, **dev):
        return pltpu.make_async_remote_copy(
            src_ref=src, dst_ref=dst, send_sem=s_sem, recv_sem=r_sem,
            device_id=dev, device_id_type=MESH,
        )

    def go(copy):
        copy.start()
        sends.append(copy)

    loads = []
    for j in range(n_out):
        for num, (src, dst) in enumerate(((sketch, sk), (right_v, rv), (right_u, ru))):
            loads.append(pltpu.make_async_copy(src.at[j], dst.at[j], load_sem.at[j, num]))
    own = pl.ds(me_co * tpd, tpd)
    own_v = pltpu.make_async_copy(left_v, vg.at[own], load_sem.at[n_out, 0])
    own_u = pltpu.make_async_copy(left_u, ug.at[own], load_sem.at[n_out, 1])
    for c in [own_v, own_u] + loads:
        c.start()

    barrier = pltpu.get_barrier_semaphore()
    for dx in range(1, nx):
        pl.semaphore_signal(barrier, inc=1, device_id={"cols": co_at(dx)}, device_id_type=MESH)
    pl.semaphore_signal(barrier, inc=1, device_id={"cols": partner}, device_id_type=MESH)
    for dy in range(1, ny):
        pl.semaphore_signal(barrier, inc=1, device_id={"inner": y_at(dy)}, device_id_type=MESH)
    for dz in range(1, nz):
        pl.semaphore_signal(barrier, inc=1, device_id={"inner": z_at(dz)}, device_id_type=MESH)
    pl.semaphore_wait(barrier, nx - 1 + 1 + ny - 1 + nz - 1)

    for num, (src, dst) in enumerate(((left_v, vg), (left_u, ug))):
        for dx in range(1, nx):
            go(remote(src, dst.at[own], gs_sem.at[num, dx], gr_sem.at[num, dx], cols=co_at(dx)))
        go(remote(src, dst.at[own], gs_sem.at[num, 0], gr_sem.at[num, 0], cols=partner))

    def block(dst, position):
        return dst.at[pl.ds(position * tpd, tpd)]

    def forward(num, dst):
        for dx in range(1, nx):
            part = block(dst, co_at(nx - dx))
            remote(part, part, gs_sem.at[num, dx], gr_sem.at[num, dx], cols=partner).wait_recv()
            go(remote(part, part, gs_sem.at[num, nx + dx], gr_sem.at[num, nx + dx], cols=partner))

    def gathered(num, dst):
        part = block(dst, partner)
        remote(part, part, gs_sem.at[num, 0], gr_sem.at[num, 0], cols=partner).wait_recv()
        for dx in range(1, nx):
            part = block(dst, lax.rem(x + nx - dx, nx) * 2 + (1 - core))
            remote(part, part, gs_sem.at[num, nx + dx], gr_sem.at[num, nx + dx], cols=partner).wait_recv()

    for c in loads:
        c.wait()
    forward(0, vg)
    gathered(0, vg)
    own_v.wait()
    own_u.wait()

    @pl.loop(0, tiles)
    def _(t):
        vt[t] = jnp.transpose(vg[t])

    for j in range(n_out):
        om = jnp.transpose(sk[j])

        @pl.loop(0, slots // 4)
        def _(quad, j=j, om=om):
            for s in [quad * 4 + i for i in range(4)]:
                live = mask[j, s].astype(F32)
                probe_hi, probe_lo = split(mm(om, rv[j, s], NN))
                pair_hi, pair_lo = split(mm(vt[lax.rem(index[j, s], tiles)], ru[j, s], NN))
                phi[j, s] = pair_hi
                plo[j, s] = pair_lo
                mixed = mm(pair_hi, probe_hi, NT) + mm(pair_hi, probe_lo, NT) + mm(pair_lo, probe_hi, NT)
                mix[j, s] = (mixed * live).astype(BF16)

        if j == 0:
            forward(1, ug)

    gathered(1, ug)

    def scatter_first(phase, j, total, buf, sb, first):
        buf[j] = total.reshape(nz, ny, rows, rk)
        low = total.astype(BF16).reshape(nz, ny, rows, rk)
        for yy in range(ny):
            sb[j, yy] = low[:, yy]
        for dy in range(1, ny):
            go(remote(
                sb.at[j, lax.rem(y + dy, ny)], first.at[j, dy],
                rs_send.at[phase, j, dy], rs_recv.at[phase, j, dy], inner=y_at(dy),
            ))

    def scatter_second(phase, j, buf, sb, first, sumf, sumb, second):
        total = buf[j, :, y]
        for dy in range(1, ny):
            part = first.at[j, dy]
            remote(part, part, rs_send.at[phase, j, dy], rs_recv.at[phase, j, dy], inner=y_at(dy)).wait_recv()
            total = total + first[j, dy].astype(F32)
        sumf[j] = total
        sumb[j] = total.astype(BF16)
        for dz in range(1, nz):
            go(remote(
                sumb.at[j, lax.rem(z + dz, nz)], second.at[j, dz],
                rs_send.at[phase, j, ny + dz], rs_recv.at[phase, j, ny + dz], inner=z_at(dz),
            ))

    def scatter_last(phase, j, sumf, second):
        total = sumf[j, z]
        for dz in range(1, nz):
            part = second.at[j, dz]
            remote(part, part, rs_send.at[phase, j, ny + dz], rs_recv.at[phase, j, ny + dz], inner=z_at(dz)).wait_recv()
            total = total + second[j, dz].astype(F32)
        return total

    for j in range(n_out):
        total = mm(ug[lax.rem(index[j, 0], tiles)], mix[j, 0], NN)
        for s in range(1, slots):
            total = total + mm(ug[lax.rem(index[j, s], tiles)], mix[j, s], NN)
        scatter_first(0, j, total, ybuf, sbuf, r1)
    for j in range(n_out):
        scatter_second(0, j, ybuf, sbuf, r1, s2f, s2b, r2)

    for j in range(n_out):
        total = scatter_last(0, j, s2f, r2)
        yrow[j] = total
        yb[j, me_in] = total.astype(BF16)
        part = yb.at[j, me_in]
        for dz in range(1, nz):
            go(remote(part, part, ag_send.at[j, 0, dz], ag_recv.at[j, 0, dz], inner=z_at(dz)))
        for dy in range(1, ny):
            go(remote(part, part, ag_send.at[j, dy, 0], ag_recv.at[j, dy, 0], inner=y_at(dy)))
    for j in range(n_out):
        for dz in range(1, nz):
            part = yb.at[j, z_at(nz - dz)]
            remote(part, part, ag_send.at[j, 0, dz], ag_recv.at[j, 0, dz], inner=z_at(dz)).wait_recv()
            for dy in range(1, ny):
                go(remote(part, part, ag_send.at[j, dy, dz], ag_recv.at[j, dy, dz], inner=y_at(dy)))

    for j in range(n_out):
        for dy in range(1, ny):
            for dz in range(nz):
                pos = lax.rem(z + nz - dz, nz) * ny + lax.rem(y + ny - dy, ny)
                part = yb.at[j, pos]
                remote(part, part, ag_send.at[j, dy, dz], ag_recv.at[j, dy, dz], inner=y_at(dy)).wait_recv()
        summed_t = jnp.transpose(yb[j].reshape(nb, rk))

        @pl.loop(0, slots // 4)
        def _(quad, j=j, summed_t=summed_t):
            for s in [quad * 4 + i for i in range(4)]:
                live = mask[j, s].astype(F32)
                z_hi, z_lo = split(mm(summed_t, ug[lax.rem(index[j, s], tiles)], NN))
                back = mm(z_hi, phi[j, s], NN) + mm(z_hi, plo[j, s], NN) + mm(z_lo, phi[j, s], NN)
                b_hi, b_lo = split(back * live)
                bt[j, s, :rk] = b_hi
                bt[j, s, rk:] = b_lo

        wide = mm(rv[j, 0], bt[j, 0], NT)
        for s in range(1, slots):
            wide = wide + mm(rv[j, s], bt[j, s], NT)
        total = wide[:, :rk] + wide[:, rk:]
        scatter_first(1, j, total, cbuf, csbuf, cr1)

    row_id = lax.broadcasted_iota(jnp.int32, (rk, rk), 0)
    col_id = lax.broadcasted_iota(jnp.int32, (rk, rk), 1)
    for j in range(n_out):
        summed = yb[j].reshape(nb, rk)
        gram = mm(summed, summed, TN)
        diag = jnp.where(row_id == col_id, gram, 0.0)
        s_row = lax.rsqrt(jnp.sum(diag, axis=0, keepdims=True))
        s_col = lax.rsqrt(jnp.sum(diag, axis=1, keepdims=True))
        scale[j] = s_row
        xm[j] = gram * s_col * s_row

    sub8 = lax.broadcasted_iota(jnp.int32, (8, rk), 0)
    lane8 = lax.broadcasted_iota(jnp.int32, (8, rk), 1)

    def eliminate(start, stop):
        @pl.loop(start, stop)
        def _(b):
            base = pl.multiple_of(b * 8, 8)
            near = lane8 - base
            at = pl.ds(base, 8)
            slabs = [xm[j, at] for j in range(n_out)]
            cols = [
                [
                    jnp.broadcast_to(jnp.sum(jnp.where(near == i, slab, 0.0), axis=1, keepdims=True), (8, rk))
                    for i in range(8)
                ]
                for slab in slabs
            ]
            pivots = [jnp.ones((8, rk), F32)] * n_out
            for k in range(8):
                hot = jnp.where(near[:1] == k, 1.0, 0.0)
                for j in range(n_out):
                    column = cols[j][k]
                    pivots[j] = jnp.where(sub8 == k, column[k : k + 1], pivots[j])
                    weight = jnp.where(sub8 > k, column * (1.0 / column[k : k + 1]), 0.0)
                    slabs[j] = slabs[j] - weight * (slabs[j][k : k + 1] + hot)
                    for i in range(k + 1, 8):
                        cols[j][i] = cols[j][i] - weight * cols[j][i][k : k + 1]
            for j in range(n_out):
                ahead = jnp.where(near >= 8, slabs[j] / pivots[j], 0.0)
                unit = jnp.where(near == sub8, 1.0, jnp.where((near >= 0) & (near > sub8) & (near < 8), 0.0, slabs[j]))
                near_all = col_id - base
                clear = (row_id - base >= 8) & (near_all >= 0) & (near_all < 8)
                xm[j] = jnp.where(clear, 0.0, xm[j]) - mm_f32(ahead, unit, TN)
                xm[j, at] = slabs[j]

    blocks = rk // 8
    eliminate(0, blocks // 2)
    for j in range(n_out):
        scatter_second(1, j, cbuf, csbuf, cr1, cs2f, cs2b, cr2)
    eliminate(blocks // 2, blocks)

    for j in range(n_out):
        work = xm[j]
        pivots = jnp.sum(jnp.where(row_id == col_id, work, 0.0), axis=1, keepdims=True)
        lower = jnp.where(col_id < row_id, work, jnp.where(row_id == col_id, 1.0, 0.0))
        inverse = lower * lax.rsqrt(pivots) * scale[j]
        basis[j] = mm_f32(yrow[j], inverse, NT) * math.sqrt(nb)
        coeff[j] = mm_f32(scatter_last(1, j, cs2f, cr2), inverse, NT)

    for copy in sends:
        copy.wait_send()


def body(n_in, n_co, left_u, left_v, right_u, right_v, sketch, tile_index, slot_mask):
    n_out, slots, nb, rk = right_u.shape
    tiles = left_u.shape[0] * n_co
    nx = n_co // 2
    ny = nx
    nz = n_in // ny
    rows = nb // n_in
    wire = [
        pltpu.VMEM((n_out, nz, ny, rows, rk), F32),
        pltpu.VMEM((n_out, ny, nz, rows, rk), BF16),
        pltpu.VMEM((n_out, ny, nz, rows, rk), BF16),
        pltpu.VMEM((n_out, nz, rows, rk), F32),
        pltpu.VMEM((n_out, nz, rows, rk), BF16),
        pltpu.VMEM((n_out, nz, rows, rk), BF16),
        pltpu.VMEM((n_out, rows, rk), F32),
    ]
    out = jax.ShapeDtypeStruct((n_out, rows, rk), F32)
    hbm = pl.BlockSpec(memory_space=pl.ANY)
    smem = pl.BlockSpec(memory_space=pltpu.SMEM)
    vmem = pl.BlockSpec(memory_space=pltpu.VMEM)
    return pl.pallas_call(
        functools.partial(kernel, n_in, n_co),
        out_shape=(out, out),
        in_specs=[hbm] * 5 + [smem] * 2,
        out_specs=(vmem, vmem),
        scratch_shapes=[
            pltpu.VMEM((tiles, nb, rk), BF16),
            pltpu.VMEM((tiles, nb, rk), BF16),
            pltpu.VMEM((tiles, rk, nb), BF16),
            pltpu.VMEM((n_out, slots, nb, rk), BF16),
            pltpu.VMEM((n_out, slots, nb, rk), BF16),
            pltpu.VMEM((n_out, nb, rk), BF16),
            pltpu.VMEM((n_out, slots, rk, rk), BF16),
            pltpu.VMEM((n_out, slots, rk, rk), BF16),
            pltpu.VMEM((n_out, slots, rk, rk), BF16),
        ]
        + wire
        + [pltpu.VMEM((n_out, n_in, rows, rk), BF16)]
        + wire
        + [
            pltpu.VMEM((n_out, rk, rk), F32),
            pltpu.VMEM((n_out, 1, rk), F32),
            pltpu.VMEM((n_out, slots, 2 * rk, rk), BF16),
            pltpu.SemaphoreType.DMA((n_out + 1, 3)),
            pltpu.SemaphoreType.DMA((2, 2 * nx)),
            pltpu.SemaphoreType.DMA((2, 2 * nx)),
            pltpu.SemaphoreType.DMA((2, n_out, ny + nz)),
            pltpu.SemaphoreType.DMA((2, n_out, ny + nz)),
            pltpu.SemaphoreType.DMA((n_out, ny, nz)),
            pltpu.SemaphoreType.DMA((n_out, ny, nz)),
        ],
        compiler_params=pltpu.CompilerParams(
            collective_id=0, has_side_effects=True, vmem_limit_bytes=60 * 1024 * 1024
        ),
    )(left_u, left_v, right_u, right_v, sketch, tile_index, slot_mask)


def solution(mesh):
    return jax.shard_map(
        functools.partial(body, mesh.shape["inner"], mesh.shape["cols"]),
        mesh=mesh,
        in_specs=(
            P(("inner", "cols"), None, None),
            P(("inner", "cols"), None, None),
            P("cols", "inner", None, None),
            P("cols", "inner", None, None),
            P("cols", None, None),
            P("cols", "inner"),
            P("cols", "inner"),
        ),
        out_specs=(P("cols", "inner", None), P("cols", "inner", None)),
        check_vma=False,
    )
```

```python
import functools
import math

import jax
import jax.numpy as jnp
from jax import lax
from jax.experimental import pallas as pl
from jax.experimental.pallas import tpu as pltpu
from jax.sharding import PartitionSpec as P

MESH = pl.DeviceIdType.MESH
F32 = jnp.float32
BF16 = jnp.bfloat16
NN = (((1,), (0,)), ((), ()))
NT = (((1,), (1,)), ((), ()))
TN = (((0,), (0,)), ((), ()))


def mm(a, b, dims):
    return lax.dot_general(a, b, dims, preferred_element_type=F32)


def split(a):
    hi = a.astype(BF16)
    return hi, (a - hi.astype(F32)).astype(BF16)


def mm_f32(a, b, dims):
    return lax.dot_general(a, b, dims, precision=lax.Precision.HIGHEST, preferred_element_type=F32)


def kernel(
    n_in, n_co, left_u, left_v, right_u, right_v, sketch, index, mask, basis, coeff,
    ug, vg, vt, ru, rv, sk, pair, probe, mix, ybuf, sbuf, r1, s2f, s2b, r2, yrow, yb,
    cbuf, csbuf, cr1, cs2f, cs2b, cr2, crow, xm, scale, bt,
    load_sem, gs_sem, gr_sem, rs_send, rs_recv, ag_send, ag_recv,
):
    nx = n_co // 2
    ny = nx
    nz = n_in // ny
    tpd = left_u.shape[0]
    tiles = tpd * n_co
    n_out, slots, nb, rk = right_u.shape
    rows = nb // n_in
    me_in = lax.axis_index("inner")
    me_co = lax.axis_index("cols")
    x, core = lax.div(me_co, 2), lax.rem(me_co, 2)
    z, y = lax.div(me_in, ny), lax.rem(me_in, ny)

    def co_at(dx):
        return lax.rem(x + dx, nx) * 2 + core

    partner = x * 2 + (1 - core)

    def z_at(dz):
        return lax.rem(z + dz, nz) * ny + y

    def y_at(dy):
        return z * ny + lax.rem(y + dy, ny)

    sends = []

    def remote(src, dst, s_sem, r_sem, **dev):
        return pltpu.make_async_remote_copy(
            src_ref=src, dst_ref=dst, send_sem=s_sem, recv_sem=r_sem,
            device_id=dev, device_id_type=MESH,
        )

    def go(copy):
        copy.start()
        sends.append(copy)

    loads = []
    for j in range(n_out):
        for num, (src, dst) in enumerate(((sketch, sk), (right_v, rv), (right_u, ru))):
            loads.append(pltpu.make_async_copy(src.at[j], dst.at[j], load_sem.at[j, num]))
    own = pl.ds(me_co * tpd, tpd)
    own_v = pltpu.make_async_copy(left_v, vg.at[own], load_sem.at[n_out, 0])
    own_u = pltpu.make_async_copy(left_u, ug.at[own], load_sem.at[n_out, 1])
    for c in [own_v, own_u] + loads:
        c.start()

    barrier = pltpu.get_barrier_semaphore()
    for dx in range(1, nx):
        pl.semaphore_signal(barrier, inc=1, device_id={"cols": co_at(dx)}, device_id_type=MESH)
    pl.semaphore_signal(barrier, inc=1, device_id={"cols": partner}, device_id_type=MESH)
    for dy in range(1, ny):
        pl.semaphore_signal(barrier, inc=1, device_id={"inner": y_at(dy)}, device_id_type=MESH)
    for dz in range(1, nz):
        pl.semaphore_signal(barrier, inc=1, device_id={"inner": z_at(dz)}, device_id_type=MESH)
    pl.semaphore_wait(barrier, nx - 1 + 1 + ny - 1 + nz - 1)

    for num, (src, dst) in enumerate(((left_v, vg), (left_u, ug))):
        for dx in range(1, nx):
            go(remote(src, dst.at[own], gs_sem.at[num, dx], gr_sem.at[num, dx], cols=co_at(dx)))
        go(remote(src, dst.at[own], gs_sem.at[num, 0], gr_sem.at[num, 0], cols=partner))

    def block(dst, position):
        return dst.at[pl.ds(position * tpd, tpd)]

    def forward(num, dst):
        for dx in range(1, nx):
            part = block(dst, co_at(nx - dx))
            remote(part, part, gs_sem.at[num, dx], gr_sem.at[num, dx], cols=partner).wait_recv()
            go(remote(part, part, gs_sem.at[num, nx + dx], gr_sem.at[num, nx + dx], cols=partner))

    def gathered(num, dst):
        part = block(dst, partner)
        remote(part, part, gs_sem.at[num, 0], gr_sem.at[num, 0], cols=partner).wait_recv()
        for dx in range(1, nx):
            part = block(dst, lax.rem(x + nx - dx, nx) * 2 + (1 - core))
            remote(part, part, gs_sem.at[num, nx + dx], gr_sem.at[num, nx + dx], cols=partner).wait_recv()

    for j in range(n_out):
        loads[3 * j].wait()
        loads[3 * j + 1].wait()
        om = jnp.transpose(sk[j])

        @pl.loop(0, slots // 4)
        def _(quad, j=j, om=om):
            for s in [quad * 4 + i for i in range(4)]:
                probe_hi, probe_lo = split(mm(om, rv[j, s], NN))
                probe[j, s, :rk] = probe_hi
                probe[j, s, rk:] = probe_lo

    forward(0, vg)
    gathered(0, vg)
    own_v.wait()

    @pl.loop(0, tiles)
    def _(t):
        vt[t] = jnp.transpose(vg[t])

    for j in range(n_out):
        loads[3 * j + 2].wait()

        @pl.loop(0, slots // 4)
        def _(quad, j=j):
            for s in [quad * 4 + i for i in range(4)]:
                live = mask[j, s].astype(F32)
                pair_hi, pair_lo = split(mm(vt[lax.rem(index[j, s], tiles)], ru[j, s], NN))
                pair[j, s, :, :rk] = pair_hi
                pair[j, s, :, rk:] = pair_lo
                wide = mm(pair_hi, probe[j, s], NT)
                mixed = wide[:, :rk] + wide[:, rk:] + mm(pair_lo, probe[j, s, :rk], NT)
                mix[j, s] = (mixed * live).astype(BF16)

        if j == n_out // 2:
            forward(1, ug)

    own_u.wait()
    gathered(1, ug)

    def scatter_first(phase, j, total, buf, sb, first):
        buf[j] = total.reshape(nz, ny, rows, rk)
        low = total.astype(BF16).reshape(nz, ny, rows, rk)
        for yy in range(ny):
            sb[j, yy] = low[:, yy]
        for dy in range(1, ny):
            go(remote(
                sb.at[j, lax.rem(y + dy, ny)], first.at[j, dy],
                rs_send.at[phase, j, dy], rs_recv.at[phase, j, dy], inner=y_at(dy),
            ))

    def scatter_second(phase, j, buf, sb, first, sumf, sumb, second):
        total = buf[j, :, y]
        for dy in range(1, ny):
            part = first.at[j, dy]
            remote(part, part, rs_send.at[phase, j, dy], rs_recv.at[phase, j, dy], inner=y_at(dy)).wait_recv()
            total = total + first[j, dy].astype(F32)
        sumf[j] = total
        sumb[j] = total.astype(BF16)
        for dz in range(1, nz):
            go(remote(
                sumb.at[j, lax.rem(z + dz, nz)], second.at[j, dz],
                rs_send.at[phase, j, ny + dz], rs_recv.at[phase, j, ny + dz], inner=z_at(dz),
            ))

    def scatter_last(phase, j, sumf, second):
        total = sumf[j, z]
        for dz in range(1, nz):
            part = second.at[j, dz]
            remote(part, part, rs_send.at[phase, j, ny + dz], rs_recv.at[phase, j, ny + dz], inner=z_at(dz)).wait_recv()
            total = total + second[j, dz].astype(F32)
        return total

    def share(j):
        total = scatter_last(0, j, s2f, r2)
        yrow[j] = total
        yb[j, me_in] = total.astype(BF16)
        part = yb.at[j, me_in]
        for dz in range(1, nz):
            go(remote(part, part, ag_send.at[j, 0, dz], ag_recv.at[j, 0, dz], inner=z_at(dz)))
        for dy in range(1, ny):
            go(remote(part, part, ag_send.at[j, dy, 0], ag_recv.at[j, dy, 0], inner=y_at(dy)))

    def relay(j):
        for dz in range(1, nz):
            part = yb.at[j, z_at(nz - dz)]
            remote(part, part, ag_send.at[j, 0, dz], ag_recv.at[j, 0, dz], inner=z_at(dz)).wait_recv()
            for dy in range(1, ny):
                go(remote(part, part, ag_send.at[j, dy, dz], ag_recv.at[j, dy, dz], inner=y_at(dy)))

    def shared(j):
        for dy in range(1, ny):
            for dz in range(nz):
                pos = lax.rem(z + nz - dz, nz) * ny + lax.rem(y + ny - dy, ny)
                part = yb.at[j, pos]
                remote(part, part, ag_send.at[j, dy, dz], ag_recv.at[j, dy, dz], inner=y_at(dy)).wait_recv()

    for j in range(n_out):
        total = mm(ug[lax.rem(index[j, 0], tiles)], mix[j, 0], NN)
        for s in range(1, slots):
            total = total + mm(ug[lax.rem(index[j, s], tiles)], mix[j, s], NN)
        scatter_first(0, j, total, ybuf, sbuf, r1)
        if j >= 1:
            scatter_second(0, j - 1, ybuf, sbuf, r1, s2f, s2b, r2)
    scatter_second(0, n_out - 1, ybuf, sbuf, r1, s2f, s2b, r2)
    for j in range(n_out):
        share(j)
        if j >= 1:
            relay(j - 1)
    relay(n_out - 1)

    row_id = lax.broadcasted_iota(jnp.int32, (rk, rk), 0)
    col_id = lax.broadcasted_iota(jnp.int32, (rk, rk), 1)
    sub8 = lax.broadcasted_iota(jnp.int32, (8, rk), 0)
    lane8 = lax.broadcasted_iota(jnp.int32, (8, rk), 1)

    def normal(j):
        summed = yb[j].reshape(nb, rk)
        gram = mm(summed, summed, TN)
        diag = jnp.where(row_id == col_id, gram, 0.0)
        s_row = lax.rsqrt(jnp.sum(diag, axis=0, keepdims=True))
        s_col = lax.rsqrt(jnp.sum(diag, axis=1, keepdims=True))
        scale[j] = s_row
        xm[j] = gram * s_col * s_row

    def eliminate(b):
        base = pl.multiple_of(b * 8, 8)
        near = lane8 - base
        at = pl.ds(base, 8)
        slabs = [xm[j, at] for j in range(n_out)]
        cols = [
            [
                jnp.broadcast_to(jnp.sum(jnp.where(near == i, slab, 0.0), axis=1, keepdims=True), (8, rk))
                for i in range(8)
            ]
            for slab in slabs
        ]
        pivots = [jnp.ones((8, rk), F32)] * n_out
        for k in range(8):
            hot = jnp.where(near[:1] == k, 1.0, 0.0)
            for j in range(n_out):
                column = cols[j][k]
                pivots[j] = jnp.where(sub8 == k, column[k : k + 1], pivots[j])
                weight = jnp.where(sub8 > k, column * (1.0 / column[k : k + 1]), 0.0)
                slabs[j] = slabs[j] - weight * (slabs[j][k : k + 1] + hot)
                for i in range(k + 1, 8):
                    cols[j][i] = cols[j][i] - weight * cols[j][i][k : k + 1]
        for j in range(n_out):
            ahead = jnp.where(near >= 8, slabs[j] / pivots[j], 0.0)
            unit = jnp.where(near == sub8, 1.0, jnp.where((near >= 0) & (near > sub8) & (near < 8), 0.0, slabs[j]))
            near_all = col_id - base
            clear = (row_id - base >= 8) & (near_all >= 0) & (near_all < 8)
            xm[j] = jnp.where(clear, 0.0, xm[j]) - mm_f32(ahead, unit, TN)
            xm[j, at] = slabs[j]

    blocks = rk // 8

    def back_slot(j, s, summed_t):
        live = mask[j, s].astype(F32)
        z_hi, z_lo = split(mm(summed_t, ug[lax.rem(index[j, s], tiles)], NN))
        wide = mm(z_hi, pair[j, s], NN)
        back = wide[:, :rk] + wide[:, rk:] + mm(z_lo, pair[j, s, :, :rk], NN)
        b_hi, b_lo = split(back * live)
        bt[j, s, :rk] = b_hi
        bt[j, s, rk:] = b_lo

    for j in range(n_out):
        shared(j)
        summed_t = jnp.transpose(yb[j].reshape(nb, rk))

        @pl.loop(0, slots // 4)
        def _(quad, j=j, summed_t=summed_t):
            for i in range(4):
                back_slot(j, quad * 4 + i, summed_t)

        wide = mm(rv[j, 0], bt[j, 0], NT)
        for s in range(1, slots):
            wide = wide + mm(rv[j, s], bt[j, s], NT)
        scatter_first(1, j, wide[:, :rk] + wide[:, rk:], cbuf, csbuf, cr1)
        if j >= 1:
            scatter_second(1, j - 1, cbuf, csbuf, cr1, cs2f, cs2b, cr2)

    for j in range(n_out):
        normal(j)

    @pl.loop(0, blocks // 4)
    def _(b):
        eliminate(b)

    scatter_second(1, n_out - 1, cbuf, csbuf, cr1, cs2f, cs2b, cr2)

    @pl.loop(blocks // 4, blocks)
    def _(b):
        eliminate(b)

    for j in range(n_out):
        work = xm[j]
        pivots = jnp.sum(jnp.where(row_id == col_id, work, 0.0), axis=1, keepdims=True)
        lower = jnp.where(col_id < row_id, work, jnp.where(row_id == col_id, 1.0, 0.0))
        inverse = lower * lax.rsqrt(pivots) * scale[j]
        basis[j] = mm_f32(yrow[j], inverse, NT) * math.sqrt(nb)
        coeff[j] = mm_f32(scatter_last(1, j, cs2f, cr2), inverse, NT)

    for copy in sends:
        copy.wait_send()


def body(n_in, n_co, left_u, left_v, right_u, right_v, sketch, tile_index, slot_mask):
    n_out, slots, nb, rk = right_u.shape
    tiles = left_u.shape[0] * n_co
    nx = n_co // 2
    ny = nx
    nz = n_in // ny
    rows = nb // n_in
    wire = [
        pltpu.VMEM((n_out, nz, ny, rows, rk), F32),
        pltpu.VMEM((n_out, ny, nz, rows, rk), BF16),
        pltpu.VMEM((n_out, ny, nz, rows, rk), BF16),
        pltpu.VMEM((n_out, nz, rows, rk), F32),
        pltpu.VMEM((n_out, nz, rows, rk), BF16),
        pltpu.VMEM((n_out, nz, rows, rk), BF16),
        pltpu.VMEM((n_out, rows, rk), F32),
    ]
    out = jax.ShapeDtypeStruct((n_out, rows, rk), F32)
    hbm = pl.BlockSpec(memory_space=pl.ANY)
    smem = pl.BlockSpec(memory_space=pltpu.SMEM)
    vmem = pl.BlockSpec(memory_space=pltpu.VMEM)
    return pl.pallas_call(
        functools.partial(kernel, n_in, n_co),
        out_shape=(out, out),
        in_specs=[hbm] * 5 + [smem] * 2,
        out_specs=(vmem, vmem),
        scratch_shapes=[
            pltpu.VMEM((tiles, nb, rk), BF16),
            pltpu.VMEM((tiles, nb, rk), BF16),
            pltpu.VMEM((tiles, rk, nb), BF16),
            pltpu.VMEM((n_out, slots, nb, rk), BF16),
            pltpu.VMEM((n_out, slots, nb, rk), BF16),
            pltpu.VMEM((n_out, nb, rk), BF16),
            pltpu.VMEM((n_out, slots, rk, 2 * rk), BF16),
            pltpu.VMEM((n_out, slots, 2 * rk, rk), BF16),
            pltpu.VMEM((n_out, slots, rk, rk), BF16),
        ]
        + wire
        + [pltpu.VMEM((n_out, n_in, rows, rk), BF16)]
        + wire
        + [
            pltpu.VMEM((n_out, rk, rk), F32),
            pltpu.VMEM((n_out, 1, rk), F32),
            pltpu.VMEM((n_out, slots, 2 * rk, rk), BF16),
            pltpu.SemaphoreType.DMA((n_out + 1, 3)),
            pltpu.SemaphoreType.DMA((2, 2 * nx)),
            pltpu.SemaphoreType.DMA((2, 2 * nx)),
            pltpu.SemaphoreType.DMA((2, n_out, ny + nz)),
            pltpu.SemaphoreType.DMA((2, n_out, ny + nz)),
            pltpu.SemaphoreType.DMA((n_out, ny, nz)),
            pltpu.SemaphoreType.DMA((n_out, ny, nz)),
        ],
        compiler_params=pltpu.CompilerParams(
            collective_id=0, has_side_effects=True, vmem_limit_bytes=60 * 1024 * 1024
        ),
    )(left_u, left_v, right_u, right_v, sketch, tile_index, slot_mask)


def solution(mesh):
    return jax.shard_map(
        functools.partial(body, mesh.shape["inner"], mesh.shape["cols"]),
        mesh=mesh,
        in_specs=(
            P(("inner", "cols"), None, None),
            P(("inner", "cols"), None, None),
            P("cols", "inner", None, None),
            P("cols", "inner", None, None),
            P("cols", None, None),
            P("cols", "inner"),
            P("cols", "inner"),
        ),
        out_specs=(P("cols", "inner", None), P("cols", "inner", None)),
        check_vma=False,
    )
```
